256 devices in a mesh: ab: 16 (over y, x), cd: 8 (over z), ij: 2 (over core).
Axes of the slice: x: 4, y: 4, z: 8, core: 2. Of those that a mesh axis runs over, the one named last changes fastest.
Arguments:
- amplitudes: float32 [512, 65536], P('ij', ('cd', 'ab')), may hold values from -6 to 6
- integrals: float32 [5888, 256, 256], P(('ab', 'cd')), may hold values from -0.375 to 0.375
- tile_row: int32 [5888], P(('ab', 'cd')), may hold values from 0 to 15, as said below
- tile_col: int32 [5888], P(('ab', 'cd')), may hold values from 0 to 31
- tile_count: int32 [128], P(('ab', 'cd')), may hold values from 1 to 46, as said below
Outputs:
- residual: float32 [512, 16, 16, 256], P('ij', 'ab', 'cd')
The draws below stay inside these ranges and needn't reach their ends.
Inputs may be any that keep to these rules, and one draw needn't show every extreme that they name: Within one slab the 46 slots name distinct (tile_row, tile_col) pairs. `tile_count`: in every draw some slab has all 46 slots live.
All inputs are finite; a program needn't handle non-finite values.
Results may differ from the reference program's by a relative error of at most 0.0003.
Values sent between devices are 32-bit elements; how exact they have to be, the bound alone decides.
No kernel may reach another device: no remote copies, remote signals or barrier semaphores. Data moves between devices by JAX's collectives and lax.ppermute only.
A program may use at most 128 MiB of HBM per device.

```python
import jax
import jax.numpy as jnp
from jax import lax

OCC_DEV = 256
BS = 16
TS = 256
NBS = 16
OCC = 512
CT_DEV = 32
KT = 46
SLABS = 128
N_AB = 16
N_CD = 8


def tile_pairs(key):
    keys = jax.random.split(jax.random.fold_in(key, 11), SLABS)
    chosen = jax.vmap(lambda one_key: jax.random.permutation(one_key, NBS * CT_DEV)[:KT])(keys)
    return chosen.reshape(-1).astype(jnp.int32)


def draw_tile_row(key, part):
    return (tile_pairs(key) // CT_DEV).astype(jnp.int32)


def draw_tile_col(key, part):
    return (tile_pairs(key) % CT_DEV).astype(jnp.int32)


def draw_tile_count(key, part):
    counts = jax.random.randint(jax.random.fold_in(key, 5), (SLABS,), 1, KT + 1)
    fullest = jax.random.randint(jax.random.fold_in(key, 6), (), 0, SLABS)
    return counts.at[fullest].set(KT).astype(jnp.int32)


def level_of(rng, extent, pieces, smallest, high):
    level = 1.0
    for dim, shards_of in pieces:
        draws = jax.random.uniform(jax.random.fold_in(jax.random.fold_in(rng, 6), dim), (shards_of,), jnp.float32, smallest / len(pieces), high / len(pieces))
        level = level * jnp.repeat(jnp.exp(draws), extent[dim] // shards_of).reshape((-1,) + (1,) * (len(extent) - 1 - dim))
    return level


def gaussian(stream_key, shape, deviation, limit, cuts=(), kind=jnp.bfloat16):
    result = deviation * jax.random.normal(stream_key, shape, jnp.float32)
    if cuts:
        result = result * level_of(stream_key, shape, cuts, -0.22, 0.18)
    return jnp.clip(result, -limit, limit).astype(kind)


def setup_inputs(seed: int = 0) -> dict:
    key_of = jax.random.split(jax.random.key(seed), 6)
    amplitudes = gaussian(key_of[0], (OCC, N_AB * N_AB * TS), 1.0, 6.0, ((0, 2), (1, 128)), jnp.float32)
    integrals = gaussian(key_of[1], (SLABS * KT, TS, TS), TS ** -0.5, 0.375, ((0, 128),), jnp.float32)
    tile_row = draw_tile_row(jax.random.fold_in(key_of[5], 71), 0)
    tile_col = draw_tile_col(jax.random.fold_in(key_of[5], 71), 0)
    tile_count = draw_tile_count(jax.random.fold_in(key_of[5], 71), 0)
    return {"amplitudes": amplitudes, "integrals": integrals, "tile_row": tile_row, "tile_col": tile_col, "tile_count": tile_count}


def reference(amplitudes, integrals, tile_row, tile_col, tile_count):
    amp_tiles = amplitudes.reshape(OCC, N_AB * N_AB, TS)
    slab_tiles = integrals.reshape(SLABS, KT, TS, TS)
    slab_rows = tile_row.reshape(SLABS, KT)
    slab_cols = tile_col.reshape(SLABS, KT)
    slab_ids = jnp.arange(SLABS, dtype=jnp.int32)

    def add_slab(total, item):
        slab_id, tiles, rows, cols, live_count = item
        ab_index = slab_id // N_CD
        cd_index = slab_id % N_CD
        chosen = jnp.take(amp_tiles, (cd_index * CT_DEV + cols).astype(jnp.int32), axis=1)
        terms = jnp.einsum("okf,kef->oke", chosen, tiles, precision=lax.Precision.HIGHEST)
        live = (jnp.arange(KT, dtype=jnp.int32) < live_count).astype(jnp.float32)
        terms = terms * live[None, :, None]
        total = total.at[:, (ab_index * NBS + rows).astype(jnp.int32), :].add(terms)
        return total, None

    start = jnp.zeros((OCC, NBS * NBS, TS), jnp.float32)
    ladder, _ = lax.scan(add_slab, start, (slab_ids, slab_tiles, slab_rows, slab_cols, tile_count))
    ladder_five = ladder.reshape(OCC, NBS, NBS, BS, BS)
    partner = jnp.roll(ladder_five, OCC_DEV, axis=0)
    mirrored = jnp.transpose(partner, (0, 2, 1, 4, 3))
    total = ladder_five + mirrored
    return jnp.transpose(total, (0, 1, 3, 2, 4)).reshape(OCC, NBS, BS, NBS * BS)
```

```python
import math

import jax
import jax.numpy as jnp
from jax import lax
from jax.experimental import pallas as pl
from jax.experimental.pallas import tpu as pltpu
from jax.sharding import PartitionSpec as P

LANES = 128
SIDE = 4


def plane_route(dx, dy):
    route = []
    for y in range(SIDE):
        for x in range(SIDE):
            route.append((y * SIDE + x, (y + dy) % SIDE * SIDE + (x + dx) % SIDE))
    return route


def shift_plane(block, dx, dy):
    return lax.ppermute(block, "ab", plane_route(dx, dy))


def both_ways(block, dx, dy):
    return [shift_plane(block, dx, dy), shift_plane(block, -dx, -dy)]


def far_halves(pair, dx, dy):
    below, above = pair
    half = below.shape[0] // 2
    return [shift_plane(below[:half], dx, dy), shift_plane(above[half:], -dx, -dy)]


def gather_plane(lower, upper, tiles):
    along_x, along_y = (1, 0), (0, 1)
    near_low = both_ways(lower, *along_x)
    near_up = both_ways(upper, *along_y)
    line_low = jnp.concatenate([lower] + near_low + far_halves(near_low, *along_x), axis=0)
    line_up = jnp.concatenate([upper] + near_up + far_halves(near_up, *along_y), axis=0)
    near_low = both_ways(line_low, *along_y)
    near_up = both_ways(line_up, *along_x)
    near_low[0], near_low[1], near_up[0], near_up[1], tiles = lax.optimization_barrier(
        (*near_low, *near_up, tiles)
    )
    far_low = far_halves(near_low, *along_y)
    far_up = far_halves(near_up, *along_x)
    return [line_low] + near_low + far_low + [line_up] + near_up + far_up, tiles


def split_kernel(tiles_ref, out_ref, left_ref, rows_ref):
    for t in range(tiles_ref.shape[0]):
        for side in range(2):
            lanes = pl.ds(side * LANES, LANES)
            left_ref[...] = tiles_ref[t, :, lanes]
            for hi in range(8):
                for a in range(2):
                    for b in range(2):
                        rows_ref[pl.ds(hi * 32 + a * 2 + b, 8, stride=4), :] = left_ref[
                            pl.ds(hi * 32 + a * 16 + b, 8, stride=2), :
                        ]
            value = rows_ref[...]
            high = value.astype(jnp.bfloat16)
            out_ref[t, 0, :, lanes] = high
            out_ref[t, 1, :, lanes] = (value - high.astype(jnp.float32)).astype(jnp.bfloat16)


def split_tiles(integrals):
    slots, size, _ = integrals.shape
    step = 2
    return pl.pallas_call(
        split_kernel,
        grid=(slots // step,),
        in_specs=[pl.BlockSpec((step, size, size), lambda k: (k, 0, 0))],
        out_specs=pl.BlockSpec((step, 2, size, size), lambda k: (k, 0, 0, 0)),
        out_shape=jax.ShapeDtypeStruct((slots, 2, size, size), jnp.bfloat16),
        scratch_shapes=[pltpu.VMEM((size, LANES), jnp.float32)] * 2,
        cost_estimate=pl.CostEstimate(
            flops=slots * size * size * 4, bytes_accessed=slots * size * size * 8, transcendentals=0
        ),
        name="split_tiles",
    )(integrals)


def place_in_line(offset):
    return jnp.where(offset == 0, 0, jnp.where(offset == 1, 2, jnp.where(offset == 2, 3, 1)))


def ladder_kernel(row_ref, col_ref, count_ref, tiles_ref, *rest):
    pieces = rest[:10]
    out_ref, amp_ref, held_ref, acc_ref, amp_sem, held_sem = rest[10:]
    size = tiles_ref.shape[-1]
    count = count_ref[0]
    copies = []
    start = 0
    for i, piece in enumerate(pieces):
        rows = piece.shape[0]
        copies.append(pltpu.make_async_copy(piece, amp_ref.at[pl.ds(start, rows)], amp_sem.at[i]))
        start += rows
    for copy in copies:
        copy.start()

    def tile_copy(k):
        return pltpu.make_async_copy(tiles_ref.at[k], held_ref.at[k], held_sem.at[k])

    def fetch(k, carry):
        tile_copy(k).start()
        return carry

    lax.fori_loop(0, count, fetch, 0)
    acc_ref[...] = jnp.zeros_like(acc_ref)
    for copy in copies:
        copy.wait()
    me = lax.axis_index("ab")
    my_y = me // SIDE
    my_x = me % SIDE

    def add_slot(k, carry):
        tile_copy(k).wait()
        row = row_ref[k]
        col = col_ref[k]
        source = col // 2
        in_x = place_in_line((source % SIDE - my_x + SIDE) % SIDE)
        in_y = place_in_line((source // SIDE - my_y + SIDE) % SIDE)
        spot = jnp.where(col % 2 == 0, in_y * SIDE + in_x, SIDE * SIDE + in_x * SIDE + in_y)
        factor = amp_ref[pl.ds(pl.multiple_of(spot * size, size), size), :]
        high = factor.astype(jnp.bfloat16)
        low = (factor - high.astype(jnp.float32)).astype(jnp.bfloat16)
        tile_high = held_ref[k, 0]
        tile_low = held_ref[k, 1]
        term = jnp.dot(tile_high, high, preferred_element_type=jnp.float32)
        term += jnp.dot(tile_high, low, preferred_element_type=jnp.float32)
        term += jnp.dot(tile_low, high, preferred_element_type=jnp.float32)
        acc_ref[row] += term
        return carry

    lax.fori_loop(0, count, add_slot, 0)

    first = lax.broadcasted_iota(jnp.int32, (8, LANES), 0) < 4

    def put(row, carry):
        for hi in range(8):
            for g in range(4):
                left = acc_ref[row, pl.ds(hi * 32 + g * 8, 8), pl.ds(0, LANES)]
                right = acc_ref[row, pl.ds(hi * 32 + g * 8, 8), pl.ds(LANES, LANES)]
                spot = pl.multiple_of(row * 64, 64)
                out_ref[hi, pl.ds(spot + g * 16, 8), :] = jnp.where(first, left, pltpu.roll(right, 4, 0))
                out_ref[hi, pl.ds(spot + g * 16 + 8, 8), :] = jnp.where(first, pltpu.roll(left, 4, 0), right)
        return carry

    lax.fori_loop(0, acc_ref.shape[0], put, 0)


def ladder(tile_row, tile_col, tile_count, tiles, pieces, blocks):
    slots, _, size, _ = tiles.shape
    width = pieces[0].shape[1]
    total = sum(piece.shape[0] for piece in pieces)
    smem = pl.BlockSpec(memory_space=pltpu.SMEM)
    hbm = pl.BlockSpec(memory_space=pl.ANY)
    return pl.pallas_call(
        ladder_kernel,
        in_specs=[smem] * 3 + [hbm] * (1 + len(pieces)),
        out_specs=pl.BlockSpec(memory_space=pltpu.VMEM),
        out_shape=jax.ShapeDtypeStruct((8, blocks * 64, LANES), jnp.float32),
        scratch_shapes=[
            pltpu.VMEM((total, width), jnp.float32),
            pltpu.VMEM((slots, 2, size, size), jnp.bfloat16),
            pltpu.VMEM((blocks, size, width), jnp.float32),
            pltpu.SemaphoreType.DMA((len(pieces),)),
            pltpu.SemaphoreType.DMA((slots,)),
        ],
        compiler_params=pltpu.CompilerParams(vmem_limit_bytes=48 * 1024 * 1024),
        cost_estimate=pl.CostEstimate(
            flops=slots * 6 * size * size * width,
            bytes_accessed=slots * size * size * 4 + total * width * 4 + blocks * size * width * 4,
            transcendentals=0,
        ),
        name="ladder",
    )(tile_row, tile_col, tile_count, tiles, *pieces)


def finish_kernel(direct_ref, mirror_ref, out_ref, rows_ref):
    for o in range(2):
        for a in range(2):
            for b in range(2):
                rows_ref[pl.ds(b, LANES, stride=2), :] = (
                    direct_ref[pl.ds(o * 4 + a * 2 + b, LANES, stride=8), :]
                    + mirror_ref[pl.ds(o * 4 + b * 2 + a, LANES, stride=8), :]
                )
            out_ref[pl.ds(o * LANES, LANES), a, :] = rows_ref[...].T


def finish(direct, mirror):
    return pl.pallas_call(
        finish_kernel,
        in_specs=[pl.BlockSpec(memory_space=pltpu.VMEM)] * 2,
        out_specs=pl.BlockSpec(memory_space=pltpu.VMEM),
        out_shape=jax.ShapeDtypeStruct((2 * LANES, 2, 2 * LANES), jnp.float32),
        scratch_shapes=[pltpu.VMEM((2 * LANES, LANES), jnp.float32)],
        name="finish",
    )(direct, mirror)


def per_device(amplitudes, integrals, tile_row, tile_col, tile_count):
    occ_dev = amplitudes.shape[0]
    tile_size = integrals.shape[1]
    blocks = lax.axis_size("ab")
    cd_size = lax.axis_size("cd")
    across = amplitudes.T
    tiles = split_tiles(integrals)
    lower, upper = across[:tile_size], across[tile_size:]
    pieces, tiles = gather_plane(lower, upper, tiles)
    partial_value = ladder(tile_row, tile_col, tile_count, tiles, pieces, blocks)
    direct = lax.psum_scatter(partial_value, "cd", scatter_dimension=0, tiled=True)
    outgoing = direct.reshape(blocks * cd_size, 8, LANES)
    arrived = lax.all_to_all(outgoing, ("ab", "cd"), split_axis=0, concat_axis=0, tiled=True)
    partner = lax.ppermute(arrived, "ij", [(0, 1), (1, 0)])
    total = finish(direct.reshape(-1, LANES), partner.reshape(-1, LANES))
    return total.reshape(occ_dev, 1, 2, 2 * LANES)


def solution(mesh):
    in_specs = (
        P("ij", ("cd", "ab")),
        P(("ab", "cd"), None, None),
        P(("ab", "cd")),
        P(("ab", "cd")),
        P(("ab", "cd")),
    )
    out_specs = P("ij", "ab", "cd", None)
    return jax.shard_map(
        per_device, mesh=mesh, in_specs=in_specs, out_specs=out_specs, check_vma=False
    )
```

```python
import functools

import jax
import jax.numpy as jnp
from jax import lax
from jax.experimental import pallas as pl
from jax.experimental.pallas import tpu as pltpu
from jax.sharding import PartitionSpec as P

LANES = 128
SIDE = 4
CHUNKS = 2
HELD = 16
GROUP = 4


def plane_route(dx, dy):
    route = []
    for y in range(SIDE):
        for x in range(SIDE):
            route.append((y * SIDE + x, (y + dy) % SIDE * SIDE + (x + dx) % SIDE))
    return route


def both_ways(block, dx, dy):
    return [
        lax.ppermute(block, "ab", plane_route(dx, dy)),
        lax.ppermute(block, "ab", plane_route(-dx, -dy)),
    ]


def far_halves(pair, dx, dy):
    below, above = pair
    half = below.shape[0] // 2
    return [
        lax.ppermute(below[:half], "ab", plane_route(dx, dy)),
        lax.ppermute(above[half:], "ab", plane_route(-dx, -dy)),
    ]


def gather_line(block, dx, dy):
    pair = both_ways(block, dx, dy)
    return pair + far_halves(pair, dx, dy)


def first_line(block, dx, dy):
    far = lax.ppermute(block, "ab", plane_route(2 * dx, 2 * dy))
    return jnp.concatenate([block] + both_ways(block, dx, dy) + [far], axis=0)


def gather_plane(block):
    half = block.shape[0] // 2
    along_x, along_y = (1, 0), (0, 1)
    low = first_line(block[:half], *along_x)
    up = first_line(block[half:], *along_y)
    return [low] + gather_line(low, *along_y) + [up] + gather_line(up, *along_x)


def place_in_line(offset):
    return jnp.where(offset == 0, 0, jnp.where(offset == 1, 2, jnp.where(offset == 2, 3, 1)))


def ladder_kernel(row_ref, col_ref, count_ref, tiles_ref, *rest, pieces_given):
    pieces = rest[:pieces_given]
    out_ref, amp_ref, held_ref, amp_sem, held_sem = rest[-5:]
    size = tiles_ref.shape[-1]
    count = count_ref[0]
    copies = []
    start = 0
    for i, piece in enumerate(pieces):
        rows = piece.shape[0]
        copies.append(pltpu.make_async_copy(piece, amp_ref.at[pl.ds(start, rows)], amp_sem.at[i]))
        start += rows
    for copy in copies:
        copy.start()

    def tile_copy(k):
        spot = lax.rem(k, HELD)
        return pltpu.make_async_copy(tiles_ref.at[k], held_ref.at[spot], held_sem.at[spot])

    def fetch(k):
        @pl.when(k < count)
        def _():
            tile_copy(k).start()

    for k in range(HELD):
        fetch(k)
    out_ref[...] = jnp.zeros_like(out_ref)
    for copy in copies:
        copy.wait()
    me = lax.axis_index("ab")
    my_y = me // SIDE
    my_x = me % SIDE

    def spot_of(col):
        if len(pieces) == 1:
            return col
        source = col // 2
        in_x = place_in_line((source % SIDE - my_x + SIDE) % SIDE)
        in_y = place_in_line((source // SIDE - my_y + SIDE) % SIDE)
        return jnp.where(col % 2 == 0, in_y * SIDE + in_x, SIDE * SIDE + in_x * SIDE + in_y)

    def split(value):
        high = value.astype(jnp.bfloat16)
        return high, (value - high.astype(jnp.float32)).astype(jnp.bfloat16)

    def term_of(k):
        spot = spot_of(col_ref[k])
        high, low = split(amp_ref[pl.ds(pl.multiple_of(spot * size, size), size), :])
        both = jnp.concatenate([high, low], axis=1)
        tile_high, tile_low = split(held_ref[lax.rem(k, HELD)])
        wide = jnp.dot(tile_high, both, preferred_element_type=jnp.float32)
        term = jnp.dot(tile_low, high, preferred_element_type=jnp.float32)
        return term + wide[:, :LANES] + wide[:, LANES:]

    def add_term(k, term):
        spot = pl.multiple_of(row_ref[k] * 32, 32)
        for hi in range(8):
            out_ref[hi, pl.ds(spot, 32), :] += term[hi * 32 : hi * 32 + 32]

    def add_group(j, carry):
        for i in range(GROUP):
            tile_copy(GROUP * j + i).wait()
        terms = [term_of(GROUP * j + i) for i in range(GROUP)]
        for i in range(GROUP):
            add_term(GROUP * j + i, terms[i])
        for i in range(GROUP):
            fetch(GROUP * j + i + HELD)
        return carry

    def add_one(k, carry):
        tile_copy(k).wait()
        add_term(k, term_of(k))
        return carry

    groups = count // GROUP
    lax.fori_loop(0, groups, add_group, 0)
    lax.fori_loop(groups * GROUP, count, add_one, 0)


def ladder(tile_row, tile_col, tile_count, after, tiles, pieces, blocks):
    slots, size, _ = tiles.shape
    total = sum(piece.shape[0] for piece in pieces)
    smem = pl.BlockSpec(memory_space=pltpu.SMEM)
    hbm = pl.BlockSpec(memory_space=pl.ANY)
    return pl.pallas_call(
        functools.partial(ladder_kernel, pieces_given=len(pieces)),
        in_specs=[smem] * 3 + [hbm] * (1 + len(pieces) + len(after)),
        out_specs=pl.BlockSpec(memory_space=pltpu.VMEM),
        out_shape=jax.ShapeDtypeStruct((8, blocks * 32, LANES), jnp.float32),
        scratch_shapes=[
            pltpu.VMEM((total, LANES), jnp.float32),
            pltpu.VMEM((HELD, size, size), jnp.float32),
            pltpu.SemaphoreType.DMA((len(pieces),)),
            pltpu.SemaphoreType.DMA((HELD,)),
        ],
        compiler_params=pltpu.CompilerParams(vmem_limit_bytes=56 * 1024 * 1024),
        cost_estimate=pl.CostEstimate(
            flops=slots * 6 * size * size * LANES,
            bytes_accessed=slots * size * size * 4 + total * LANES * 4 + blocks * size * LANES * 4,
            transcendentals=0,
        ),
        name="ladder",
    )(tile_row, tile_col, tile_count, tiles, *pieces, *after)


def shift_line(block, step):
    size = lax.axis_size("cd")
    return lax.ppermute(block, "cd", [(i, (i + step) % size) for i in range(size)])


def ring_terms(partial_value):
    size = lax.axis_size("cd")
    me = lax.axis_index("cd")
    half = partial_value.shape[1] // 2

    def block_for(distance):
        return lax.dynamic_index_in_dim(
            partial_value, lax.rem(me + (distance + size), size), 0, False, allow_negative_indices=False
        )

    far = block_for(size // 2)
    up = shift_line(far[:half], 1)
    down = shift_line(far[half:], -1)
    for distance in range(size // 2 - 1, 0, -1):
        ahead = block_for(distance)
        behind = block_for(-distance)
        if distance == size // 2 - 1:
            up = jnp.concatenate([ahead[:half] + up, ahead[half:]], axis=0)
            down = jnp.concatenate([behind[:half], behind[half:] + down], axis=0)
        else:
            up = ahead + up
            down = behind + down
        up = shift_line(up, 1)
        down = shift_line(down, -1)
    return [up, down, block_for(0)], [partial_value]


def merge_kernel(*refs, terms):
    out_ref, held_ref = refs[-2:]
    start = 0
    for c in range(CHUNKS):
        value = refs[start][...]
        for ref in refs[start + 1 : start + terms[c]]:
            value = value + ref[...]
        start += terms[c]
        held_ref[...] = value
        for row in range(held_ref.shape[0] // 32):
            for a in range(2):
                for b in range(2):
                    out_ref[pl.ds(row * 64 + c * 4 + a * 2 + b, 8, stride=8), :] = held_ref[
                        pl.ds(row * 32 + a * 16 + b, 8, stride=2), :
                    ]


def merge(chunks):
    rows = chunks[0][0].shape[0]
    flat = [term for terms in chunks for term in terms]
    return pl.pallas_call(
        functools.partial(merge_kernel, terms=[len(terms) for terms in chunks]),
        in_specs=[pl.BlockSpec(memory_space=pltpu.VMEM)] * len(flat),
        out_specs=pl.BlockSpec(memory_space=pltpu.VMEM),
        out_shape=jax.ShapeDtypeStruct((CHUNKS * rows, LANES), jnp.float32),
        scratch_shapes=[pltpu.VMEM((rows, LANES), jnp.float32)],
        name="merge",
    )(*flat)


def finish_kernel(direct_ref, mirror_ref, out_ref, rows_ref):
    for o in range(CHUNKS):
        for a in range(2):
            for b in range(2):
                rows_ref[pl.ds(b, LANES, stride=2), :] = (
                    direct_ref[pl.ds(o * 4 + a * 2 + b, LANES, stride=8), :]
                    + mirror_ref[pl.ds(o * 4 + b * 2 + a, LANES, stride=8), :]
                )
            out_ref[pl.ds(o * LANES, LANES), a, :] = rows_ref[...].T


def finish(direct, mirror):
    return pl.pallas_call(
        finish_kernel,
        in_specs=[pl.BlockSpec(memory_space=pltpu.VMEM)] * 2,
        out_specs=pl.BlockSpec(memory_space=pltpu.VMEM),
        out_shape=jax.ShapeDtypeStruct((CHUNKS * LANES, 2, 2 * LANES), jnp.float32),
        scratch_shapes=[pltpu.VMEM((2 * LANES, LANES), jnp.float32)],
        name="finish",
    )(direct, mirror)


def per_device(amplitudes, integrals, tile_row, tile_col, tile_count):
    occ_dev = amplitudes.shape[0]
    blocks = lax.axis_size("ab")

    def partial_of(pieces, after):
        return ladder(tile_row, tile_col, tile_count, after, integrals, pieces, blocks)

    first, second = amplitudes[:LANES].T, amplitudes[LANES:].T
    pieces = [lax.all_gather(second, "ab", axis=0, tiled=True)]
    terms, after = ring_terms(partial_of(gather_plane(first), []))
    summed = lax.psum_scatter(partial_of(pieces, after), "cd", scatter_dimension=0, tiled=True)
    direct = merge([terms, [summed[0]]])
    outgoing = direct.reshape(-1, 8, LANES)
    arrived = lax.all_to_all(outgoing, ("ab", "cd"), split_axis=0, concat_axis=0, tiled=True)
    partner = lax.ppermute(arrived, "ij", [(0, 1), (1, 0)]).reshape(direct.shape)
    return finish(direct, partner).reshape(occ_dev, 1, 2, 2 * LANES)


def solution(mesh):
    in_specs = (
        P("ij", ("cd", "ab")),
        P(("ab", "cd"), None, None),
        P(("ab", "cd")),
        P(("ab", "cd")),
        P(("ab", "cd")),
    )
    out_specs = P("ij", "ab", "cd", None)
    return jax.shard_map(
        per_device, mesh=mesh, in_specs=in_specs, out_specs=out_specs, check_vma=False
    )
```

```python
import functools

import jax
import jax.numpy as jnp
from jax import lax
from jax.experimental import pallas as pl
from jax.experimental.pallas import tpu as pltpu
from jax.sharding import PartitionSpec as P

LANES = 128
SIDE = 4
CHUNKS = 2
HELD = 16
GROUP = 2


def plane_route(dx, dy):
    route = []
    for y in range(SIDE):
        for x in range(SIDE):
            route.append((y * SIDE + x, (y + dy) % SIDE * SIDE + (x + dx) % SIDE))
    return route


def both_ways(block, dx, dy):
    return [
        lax.ppermute(block, "ab", plane_route(dx, dy)),
        lax.ppermute(block, "ab", plane_route(-dx, -dy)),
    ]


def far_halves(pair, dx, dy):
    below, above = pair
    half = below.shape[0] // 2
    return [
        lax.ppermute(below[:half], "ab", plane_route(dx, dy)),
        lax.ppermute(above[half:], "ab", plane_route(-dx, -dy)),
    ]


def first_line(block, dx, dy):
    far = lax.ppermute(block, "ab", plane_route(2 * dx, 2 * dy))
    return jnp.concatenate([block] + both_ways(block, dx, dy) + [far], axis=0)


def gather_plane(block):
    half = block.shape[0] // 2
    along_x, along_y = (1, 0), (0, 1)
    low = first_line(block[:half], *along_x)
    up = first_line(block[half:], *along_y)
    near_low = both_ways(low, *along_y)
    near_up = both_ways(up, *along_x)
    pieces = [low] + near_low + far_halves(near_low, *along_y)
    return pieces + [up] + near_up + far_halves(near_up, *along_x)


def place_in_line(offset):
    return jnp.where(offset == 0, 0, jnp.where(offset == 1, 2, jnp.where(offset == 2, 3, 1)))


def out_parts(rows, size):
    half = rows // 2
    parts = [(size // 2, 0, half), (size // 2, half, half)]
    for distance in range(size // 2 - 1, 0, -1):
        parts += [(distance, 0, rows), (-distance, 0, rows)]
    return parts + [(0, 0, rows)]


def ladder_kernel(row_ref, col_ref, count_ref, tiles_ref, *rest, pieces_given, outs_given):
    pieces = rest[:pieces_given]
    outs = rest[pieces_given : pieces_given + outs_given]
    amp_ref, held_ref, acc_ref, amp_sem, held_sem, out_sem = rest[pieces_given + outs_given :]
    size = tiles_ref.shape[-1]
    count = count_ref[0]
    copies = []
    start = 0
    for i, piece in enumerate(pieces):
        rows = piece.shape[0]
        copies.append(pltpu.make_async_copy(piece, amp_ref.at[pl.ds(start, rows)], amp_sem.at[i]))
        start += rows
    for copy in copies:
        copy.start()

    def tile_copy(k):
        spot = lax.rem(k, HELD)
        return pltpu.make_async_copy(tiles_ref.at[k], held_ref.at[spot], held_sem.at[spot])

    def fetch(k):
        @pl.when(k < count)
        def _():
            tile_copy(k).start()

    for k in range(HELD):
        fetch(k)
    acc_ref[...] = jnp.zeros_like(acc_ref)
    for copy in copies:
        copy.wait()
    me = lax.axis_index("ab")
    my_y = me // SIDE
    my_x = me % SIDE

    def spot_of(col):
        source = col // 2
        in_x = place_in_line((source % SIDE - my_x + SIDE) % SIDE)
        in_y = place_in_line((source // SIDE - my_y + SIDE) % SIDE)
        return jnp.where(col % 2 == 0, in_y * SIDE + in_x, SIDE * SIDE + in_x * SIDE + in_y)

    def split(value):
        high = value.astype(jnp.bfloat16)
        return high, (value - high.astype(jnp.float32)).astype(jnp.bfloat16)

    def term_of(k):
        spot = spot_of(col_ref[k])
        high, low = split(amp_ref[pl.ds(pl.multiple_of(spot * size, size), size), :])
        tile_high, tile_low = split(held_ref[lax.rem(k, HELD)])
        term = jnp.dot(tile_high, high, preferred_element_type=jnp.float32)
        term += jnp.dot(tile_high, low, preferred_element_type=jnp.float32)
        return term + jnp.dot(tile_low, high, preferred_element_type=jnp.float32)

    def add_term(k, term):
        spot = pl.multiple_of(row_ref[k] * 32, 32)
        for hi in range(8):
            for c in range(CHUNKS):
                acc_ref[c, hi, pl.ds(spot, 32), :] += term[
                    hi * 32 : hi * 32 + 32, c * LANES : (c + 1) * LANES
                ]

    def add_group(j, carry):
        for i in range(GROUP):
            tile_copy(GROUP * j + i).wait()
        terms = [term_of(GROUP * j + i) for i in range(GROUP)]
        for i in range(GROUP):
            add_term(GROUP * j + i, terms[i])
        for i in range(GROUP):
            fetch(GROUP * j + i + HELD)
        return carry

    def add_one(k, carry):
        tile_copy(k).wait()
        add_term(k, term_of(k))
        return carry

    groups = count // GROUP
    lax.fori_loop(0, groups, add_group, 0)
    lax.fori_loop(groups * GROUP, count, add_one, 0)

    me_cd = lax.axis_index("cd")
    size_cd = acc_ref.shape[1]
    parts = out_parts(acc_ref.shape[2], size_cd)
    copies = []
    for i, (distance, first, rows) in enumerate(parts):
        block = lax.rem(me_cd + (distance + size_cd), size_cd)
        for c in range(CHUNKS):
            spot = c * len(parts) + i
            source = acc_ref.at[c, block, pl.ds(first, rows)]
            copies.append(pltpu.make_async_copy(source, outs[spot], out_sem.at[spot]))
    for copy in copies:
        copy.start()
    for copy in copies:
        copy.wait()


def ladder(tile_row, tile_col, tile_count, tiles, pieces, blocks):
    slots, size, _ = tiles.shape
    width = pieces[0].shape[1]
    total = sum(piece.shape[0] for piece in pieces)
    size_cd = lax.axis_size("cd")
    parts = out_parts(blocks * 32, size_cd)
    smem = pl.BlockSpec(memory_space=pltpu.SMEM)
    hbm = pl.BlockSpec(memory_space=pl.ANY)
    outs = [jax.ShapeDtypeStruct((rows, LANES), jnp.float32) for _, _, rows in parts] * CHUNKS
    given = pl.pallas_call(
        functools.partial(ladder_kernel, pieces_given=len(pieces), outs_given=len(outs)),
        in_specs=[smem] * 3 + [hbm] * (1 + len(pieces)),
        out_specs=[hbm] * len(outs),
        out_shape=outs,
        scratch_shapes=[
            pltpu.VMEM((total, width), jnp.float32),
            pltpu.VMEM((HELD, size, size), jnp.float32),
            pltpu.VMEM((CHUNKS, size_cd, blocks * 32, LANES), jnp.float32),
            pltpu.SemaphoreType.DMA((len(pieces),)),
            pltpu.SemaphoreType.DMA((HELD,)),
            pltpu.SemaphoreType.DMA((len(outs),)),
        ],
        compiler_params=pltpu.CompilerParams(vmem_limit_bytes=56 * 1024 * 1024),
        cost_estimate=pl.CostEstimate(
            flops=slots * 6 * size * size * width,
            bytes_accessed=slots * size * size * 4 + total * width * 4 + blocks * size * width * 4,
            transcendentals=0,
        ),
        name="ladder",
    )(tile_row, tile_col, tile_count, tiles, *pieces)
    return [given[c * len(parts) : (c + 1) * len(parts)] for c in range(CHUNKS)]


def shift_line(block, step):
    size = lax.axis_size("cd")
    return lax.ppermute(block, "cd", [(i, (i + step) % size) for i in range(size)])


def ring_terms(given):
    up, down = shift_line(given[0], 1), shift_line(given[1], -1)
    half = up.shape[0]
    for step in range(2, len(given) - 1, 2):
        ahead, behind = given[step : step + 2]
        if step == 2:
            up = jnp.concatenate([ahead[:half] + up, ahead[half:]], axis=0)
            down = jnp.concatenate([behind[:half], behind[half:] + down], axis=0)
        else:
            up = ahead + up
            down = behind + down
        up = shift_line(up, 1)
        down = shift_line(down, -1)
    return [up, down, given[-1]]


def bring(refs, held_ref, sem):
    copies = [pltpu.make_async_copy(ref, held_ref.at[i], sem.at[i]) for i, ref in enumerate(refs)]
    for copy in copies:
        copy.start()
    for copy in copies:
        copy.wait()


def merge_kernel(*refs, terms):
    out_ref, held_ref, terms_ref, sem = refs[-4:]
    bring(refs[:-4], terms_ref, sem)
    start = 0
    for c in range(CHUNKS):
        value = terms_ref[start]
        for i in range(start + 1, start + terms[c]):
            value = value + terms_ref[i]
        start += terms[c]
        held_ref[...] = value
        for row in range(held_ref.shape[0] // 32):
            for a in range(2):
                for b in range(2):
                    out_ref[pl.ds(row * 64 + c * 4 + a * 2 + b, 8, stride=8), :] = held_ref[
                        pl.ds(row * 32 + a * 16 + b, 8, stride=2), :
                    ]


def merge(chunks):
    rows = chunks[0][0].shape[0]
    flat = [term for terms in chunks for term in terms]
    return pl.pallas_call(
        functools.partial(merge_kernel, terms=[len(terms) for terms in chunks]),
        in_specs=[pl.BlockSpec(memory_space=pl.ANY)] * len(flat),
        out_specs=pl.BlockSpec(memory_space=pltpu.VMEM),
        out_shape=jax.ShapeDtypeStruct((CHUNKS * rows, LANES), jnp.float32),
        scratch_shapes=[
            pltpu.VMEM((rows, LANES), jnp.float32),
            pltpu.VMEM((len(flat), rows, LANES), jnp.float32),
            pltpu.SemaphoreType.DMA((len(flat),)),
        ],
        name="merge",
    )(*flat)


def finish_kernel(direct_any, mirror_any, out_ref, rows_ref, held_ref, sem):
    bring([direct_any, mirror_any], held_ref, sem)
    direct_ref, mirror_ref = held_ref.at[0], held_ref.at[1]
    for o in range(CHUNKS):
        for a in range(2):
            for b in range(2):
                rows_ref[pl.ds(b, LANES, stride=2), :] = (
                    direct_ref[pl.ds(o * 4 + a * 2 + b, LANES, stride=8), :]
                    + mirror_ref[pl.ds(o * 4 + b * 2 + a, LANES, stride=8), :]
                )
            out_ref[pl.ds(o * LANES, LANES), a, :] = rows_ref[...].T


def finish(direct, mirror):
    return pl.pallas_call(
        finish_kernel,
        in_specs=[pl.BlockSpec(memory_space=pl.ANY)] * 2,
        out_specs=pl.BlockSpec(memory_space=pltpu.VMEM),
        out_shape=jax.ShapeDtypeStruct((CHUNKS * LANES, 2, 2 * LANES), jnp.float32),
        scratch_shapes=[
            pltpu.VMEM((2 * LANES, LANES), jnp.float32),
            pltpu.VMEM((2, *direct.shape), jnp.float32),
            pltpu.SemaphoreType.DMA((2,)),
        ],
        name="finish",
    )(direct, mirror)


def per_device(amplitudes, integrals, tile_row, tile_col, tile_count):
    occ_dev = amplitudes.shape[0]
    blocks = lax.axis_size("ab")

    pieces = gather_plane(amplitudes.T)
    given = ladder(tile_row, tile_col, tile_count, integrals, pieces, blocks)
    sums = [ring_terms(blocks_of) for blocks_of in given]
    direct = merge(sums)
    outgoing = direct.reshape(-1, 8, LANES)
    arrived = lax.all_to_all(outgoing, ("ab", "cd"), split_axis=0, concat_axis=0, tiled=True)
    partner = lax.ppermute(arrived, "ij", [(0, 1), (1, 0)]).reshape(direct.shape)
    return finish(direct, partner).reshape(occ_dev, 1, 2, 2 * LANES)


def solution(mesh):
    in_specs = (
        P("ij", ("cd", "ab")),
        P(("ab", "cd"), None, None),
        P(("ab", "cd")),
        P(("ab", "cd")),
        P(("ab", "cd")),
    )
    out_specs = P("ij", "ab", "cd", None)
    return jax.shard_map(
        per_device, mesh=mesh, in_specs=in_specs, out_specs=out_specs, check_vma=False
    )
```

```python
import functools

import jax
import jax.numpy as jnp
from jax import lax
from jax.experimental import pallas as pl
from jax.experimental.pallas import tpu as pltpu
from jax.sharding import PartitionSpec as P

LANES = 128
SIDE = 4
CHUNKS = 2
HELD = 16
GROUP = 2


def plane_route(dx, dy):
    route = []
    for y in range(SIDE):
        for x in range(SIDE):
            route.append((y * SIDE + x, (y + dy) % SIDE * SIDE + (x + dx) % SIDE))
    return route


def both_ways(block, dx, dy):
    return [
        lax.ppermute(block, "ab", plane_route(dx, dy)),
        lax.ppermute(block, "ab", plane_route(-dx, -dy)),
    ]


def far_halves(pair, dx, dy):
    below, above = pair
    half = below.shape[0] // 2
    return [
        lax.ppermute(below[:half], "ab", plane_route(dx, dy)),
        lax.ppermute(above[half:], "ab", plane_route(-dx, -dy)),
    ]


def first_line(block, dx, dy):
    far = lax.ppermute(block, "ab", plane_route(2 * dx, 2 * dy))
    return jnp.concatenate([block] + both_ways(block, dx, dy) + [far], axis=0)


def gather_plane(block):
    half = block.shape[0] // 2
    along_x, along_y = (1, 0), (0, 1)
    low = first_line(block[:half], *along_x)
    up = first_line(block[half:], *along_y)
    near_low = both_ways(low, *along_y)
    near_up = both_ways(up, *along_x)
    far = far_halves(near_low, *along_y) + far_halves(near_up, *along_x)
    return [low] + near_low + [up] + near_up, far


def out_parts(rows, size):
    half = rows // 2
    parts = [(size // 2, 0, half), (size // 2, half, half)]
    for distance in range(size // 2 - 1, 0, -1):
        parts += [(distance, 0, rows), (-distance, 0, rows)]
    return parts + [(0, 0, rows)]


def ladder_kernel(row_ref, col_ref, count_ref, tiles_ref, *rest, pieces_given, last):
    pieces = rest[:pieces_given]
    outs = rest[pieces_given + last : -9]
    amp_ref, held_ref, acc_ref, slot_ref, place_ref, amp_sem, held_sem, out_sem, acc_sem = rest[-9:]
    size = tiles_ref.shape[-1]
    lines = 1 if last else SIDE - 1
    copies = []
    if last:
        copies.append(pltpu.make_async_copy(rest[pieces_given], acc_ref, acc_sem))
    start = 0
    for i, piece in enumerate(pieces):
        rows = piece.shape[0]
        copies.append(pltpu.make_async_copy(piece, amp_ref.at[pl.ds(start, rows)], amp_sem.at[i]))
        start += rows
    for copy in copies:
        copy.start()

    me = lax.axis_index("ab")
    my_y = me >> 2
    my_x = me & 3

    def pick(k, found):
        col = col_ref[k]
        in_x = (120 >> (2 * (((col >> 1) - my_x) & 3))) & 3
        in_y = (120 >> (2 * (((col >> 3) - my_y) & 3))) & 3
        odd = col & 1
        line = jnp.where(odd == 0, in_y, in_x)
        spot = jnp.where(odd == 0, in_x, in_y)
        slot_ref[found] = k
        if last:
            place_ref[found] = odd * SIDE + spot
            return found + jnp.where(line == SIDE - 1, 1, 0)
        place_ref[found] = (odd * lines + line) * SIDE + spot
        return found + jnp.where(line == SIDE - 1, 0, 1)

    count = lax.fori_loop(0, count_ref[0], pick, 0)

    def tile_copy(j):
        spot = lax.rem(j, HELD)
        return pltpu.make_async_copy(tiles_ref.at[slot_ref[j]], held_ref.at[spot], held_sem.at[spot])

    def fetch(j):
        @pl.when(j < count)
        def _():
            tile_copy(j).start()

    for j in range(HELD):
        fetch(j)
    if not last:
        acc_ref[...] = jnp.zeros_like(acc_ref)
    for copy in copies:
        copy.wait()

    def split(value):
        high = value.astype(jnp.bfloat16)
        return high, (value - high.astype(jnp.float32)).astype(jnp.bfloat16)

    def term_of(j):
        high, low = split(amp_ref[pl.ds(pl.multiple_of(place_ref[j] * size, size), size), :])
        tile_high, tile_low = split(held_ref[lax.rem(j, HELD)])
        term = jnp.dot(tile_high, high, preferred_element_type=jnp.float32)
        term += jnp.dot(tile_high, low, preferred_element_type=jnp.float32)
        return term + jnp.dot(tile_low, high, preferred_element_type=jnp.float32)

    def add_term(j, term):
        spot = pl.multiple_of(row_ref[slot_ref[j]] * 32, 32)
        for hi in range(8):
            for c in range(CHUNKS):
                acc_ref[c, hi, pl.ds(spot, 32), :] += term[
                    hi * 32 : hi * 32 + 32, c * LANES : (c + 1) * LANES
                ]

    def add_group(g, carry):
        for i in range(GROUP):
            tile_copy(GROUP * g + i).wait()
        terms = [term_of(GROUP * g + i) for i in range(GROUP)]
        for i in range(GROUP):
            add_term(GROUP * g + i, terms[i])
        for i in range(GROUP):
            fetch(GROUP * g + i + HELD)
        return carry

    def add_one(j, carry):
        tile_copy(j).wait()
        add_term(j, term_of(j))
        return carry

    groups = count // GROUP
    lax.fori_loop(0, groups, add_group, 0)
    lax.fori_loop(groups * GROUP, count, add_one, 0)

    if not last:
        copy = pltpu.make_async_copy(acc_ref, outs[0], acc_sem)
        copy.start()
        copy.wait()
        return
    me_cd = lax.axis_index("cd")
    size_cd = acc_ref.shape[1]
    parts = out_parts(acc_ref.shape[2], size_cd)
    copies = []
    for i, (distance, first, rows) in enumerate(parts):
        block = lax.rem(me_cd + (distance + size_cd), size_cd)
        for c in range(CHUNKS):
            spot = c * len(parts) + i
            source = acc_ref.at[c, block, pl.ds(first, rows)]
            copies.append(pltpu.make_async_copy(source, outs[spot], out_sem.at[spot]))
    for copy in copies:
        copy.start()
    for copy in copies:
        copy.wait()


def ladder(tile_row, tile_col, tile_count, tiles, pieces, so_far, blocks):
    slots, size, _ = tiles.shape
    width = pieces[0].shape[1]
    total = sum(piece.shape[0] for piece in pieces)
    size_cd = lax.axis_size("cd")
    smem = pl.BlockSpec(memory_space=pltpu.SMEM)
    hbm = pl.BlockSpec(memory_space=pl.ANY)
    acc = (CHUNKS, size_cd, blocks * 32, LANES)
    if so_far:
        outs = [(rows, LANES) for _, _, rows in out_parts(blocks * 32, size_cd)] * CHUNKS
    else:
        outs = [acc]
    share = total / (2 * SIDE * SIDE * size)
    return pl.pallas_call(
        functools.partial(ladder_kernel, pieces_given=len(pieces), last=len(so_far)),
        in_specs=[smem] * 3 + [hbm] * (1 + len(pieces) + len(so_far)),
        out_specs=[hbm] * len(outs),
        out_shape=[jax.ShapeDtypeStruct(shape, jnp.float32) for shape in outs],
        scratch_shapes=[
            pltpu.VMEM((total, width), jnp.float32),
            pltpu.VMEM((HELD, size, size), jnp.float32),
            pltpu.VMEM(acc, jnp.float32),
            pltpu.SMEM((slots,), jnp.int32),
            pltpu.SMEM((slots,), jnp.int32),
            pltpu.SemaphoreType.DMA((len(pieces),)),
            pltpu.SemaphoreType.DMA((HELD,)),
            pltpu.SemaphoreType.DMA((len(outs),)),
            pltpu.SemaphoreType.DMA,
        ],
        compiler_params=pltpu.CompilerParams(vmem_limit_bytes=56 * 1024 * 1024),
        cost_estimate=pl.CostEstimate(
            flops=int(share * slots * 6 * size * size * width),
            bytes_accessed=int(share * slots * size * size * 4)
            + total * width * 4
            + (1 + len(so_far)) * blocks * size * width * 4,
            transcendentals=0,
        ),
        name="ladder_last" if so_far else "ladder",
    )(tile_row, tile_col, tile_count, tiles, *pieces, *so_far)


def shift_line(block, step):
    size = lax.axis_size("cd")
    return lax.ppermute(block, "cd", [(i, (i + step) % size) for i in range(size)])


def ring_terms(given):
    up, down = shift_line(given[0], 1), shift_line(given[1], -1)
    half = up.shape[0]
    for step in range(2, len(given) - 1, 2):
        ahead, behind = given[step : step + 2]
        if step == 2:
            up = jnp.concatenate([ahead[:half] + up, ahead[half:]], axis=0)
            down = jnp.concatenate([behind[:half], behind[half:] + down], axis=0)
        else:
            up = ahead + up
            down = behind + down
        up = shift_line(up, 1)
        down = shift_line(down, -1)
    return [up, down, given[-1]]


def bring(refs, held_ref, sem):
    copies = [pltpu.make_async_copy(ref, held_ref.at[i], sem.at[i]) for i, ref in enumerate(refs)]
    for copy in copies:
        copy.start()
    for copy in copies:
        copy.wait()


def merge_kernel(*refs, terms):
    out_ref, held_ref, terms_ref, sem = refs[-4:]
    bring(refs[:-4], terms_ref, sem)
    start = 0
    for c in range(CHUNKS):
        value = terms_ref[start]
        for i in range(start + 1, start + terms[c]):
            value = value + terms_ref[i]
        start += terms[c]
        held_ref[...] = value
        for row in range(held_ref.shape[0] // 32):
            for a in range(2):
                for b in range(2):
                    out_ref[pl.ds(row * 64 + c * 4 + a * 2 + b, 8, stride=8), :] = held_ref[
                        pl.ds(row * 32 + a * 16 + b, 8, stride=2), :
                    ]


def merge(chunks):
    rows = chunks[0][0].shape[0]
    flat = [term for terms in chunks for term in terms]
    return pl.pallas_call(
        functools.partial(merge_kernel, terms=[len(terms) for terms in chunks]),
        in_specs=[pl.BlockSpec(memory_space=pl.ANY)] * len(flat),
        out_specs=pl.BlockSpec(memory_space=pltpu.VMEM),
        out_shape=jax.ShapeDtypeStruct((CHUNKS * rows, LANES), jnp.float32),
        scratch_shapes=[
            pltpu.VMEM((rows, LANES), jnp.float32),
            pltpu.VMEM((len(flat), rows, LANES), jnp.float32),
            pltpu.SemaphoreType.DMA((len(flat),)),
        ],
        name="merge",
    )(*flat)


def finish_kernel(direct_any, mirror_any, out_ref, rows_ref, held_ref, sem):
    bring([direct_any, mirror_any], held_ref, sem)
    direct_ref, mirror_ref = held_ref.at[0], held_ref.at[1]
    for o in range(CHUNKS):
        for a in range(2):
            for b in range(2):
                rows_ref[pl.ds(b, LANES, stride=2), :] = (
                    direct_ref[pl.ds(o * 4 + a * 2 + b, LANES, stride=8), :]
                    + mirror_ref[pl.ds(o * 4 + b * 2 + a, LANES, stride=8), :]
                )
            out_ref[pl.ds(o * LANES, LANES), a, :] = rows_ref[...].T


def finish(direct, mirror):
    return pl.pallas_call(
        finish_kernel,
        in_specs=[pl.BlockSpec(memory_space=pl.ANY)] * 2,
        out_specs=pl.BlockSpec(memory_space=pltpu.VMEM),
        out_shape=jax.ShapeDtypeStruct((CHUNKS * LANES, 2, 2 * LANES), jnp.float32),
        scratch_shapes=[
            pltpu.VMEM((2 * LANES, LANES), jnp.float32),
            pltpu.VMEM((2, *direct.shape), jnp.float32),
            pltpu.SemaphoreType.DMA((2,)),
        ],
        name="finish",
    )(direct, mirror)


def per_device(amplitudes, integrals, tile_row, tile_col, tile_count):
    occ_dev = amplitudes.shape[0]
    blocks = lax.axis_size("ab")

    near, far = gather_plane(amplitudes.T)
    so_far = ladder(tile_row, tile_col, tile_count, integrals, near, [], blocks)
    given = ladder(tile_row, tile_col, tile_count, integrals, far, so_far, blocks)
    each = len(given) // CHUNKS
    sums = [ring_terms(given[c * each : (c + 1) * each]) for c in range(CHUNKS)]
    direct = merge(sums)
    outgoing = direct.reshape(-1, 8, LANES)
    arrived = lax.all_to_all(outgoing, ("ab", "cd"), split_axis=0, concat_axis=0, tiled=True)
    partner = lax.ppermute(arrived, "ij", [(0, 1), (1, 0)]).reshape(direct.shape)
    return finish(direct, partner).reshape(occ_dev, 1, 2, 2 * LANES)


def solution(mesh):
    in_specs = (
        P("ij", ("cd", "ab")),
        P(("ab", "cd"), None, None),
        P(("ab", "cd")),
        P(("ab", "cd")),
        P(("ab", "cd")),
    )
    out_specs = P("ij", "ab", "cd", None)
    return jax.shard_map(
        per_device, mesh=mesh, in_specs=in_specs, out_specs=out_specs, check_vma=False
    )
```

```python
import functools

import jax
import jax.numpy as jnp
from jax import lax
from jax.experimental import pallas as pl
from jax.experimental.pallas import tpu as pltpu
from jax.sharding import PartitionSpec as P

LANES = 128
SIDE = 4
CHUNKS = 2
HELD = 16
GROUP = 2


def plane_route(dx, dy):
    route = []
    for y in range(SIDE):
        for x in range(SIDE):
            route.append((y * SIDE + x, (y + dy) % SIDE * SIDE + (x + dx) % SIDE))
    return route


def both_ways(block, dx, dy):
    return [
        lax.ppermute(block, "ab", plane_route(dx, dy)),
        lax.ppermute(block, "ab", plane_route(-dx, -dy)),
    ]


def far_halves(pair, dx, dy):
    below, above = pair
    half = below.shape[0] // 2
    return [
        lax.ppermute(below[:half], "ab", plane_route(dx, dy)),
        lax.ppermute(above[half:], "ab", plane_route(-dx, -dy)),
    ]


def first_line(block, dx, dy):
    far = lax.ppermute(block, "ab", plane_route(2 * dx, 2 * dy))
    return jnp.concatenate([block] + both_ways(block, dx, dy) + [far], axis=0)


def gather_plane(block):
    half = block.shape[0] // 2
    along_x, along_y = (1, 0), (0, 1)
    low = first_line(block[:half], *along_x)
    up = first_line(block[half:], *along_y)
    near_low = both_ways(low, *along_y)
    near_up = both_ways(up, *along_x)
    far = far_halves(near_low, *along_y) + far_halves(near_up, *along_x)
    return [low] + near_low + [up] + near_up, far


def out_parts(rows, size):
    half = rows // 2
    parts = [(size // 2, 0, half), (size // 2, half, half)]
    for distance in range(size // 2 - 1, 0, -1):
        parts += [(distance, 0, rows), (-distance, 0, rows)]
    return parts + [(0, 0, rows)]


def ladder_kernel(row_ref, col_ref, count_ref, tiles_ref, *rest, pieces_given, last):
    pieces = rest[:pieces_given]
    outs = rest[pieces_given + last : -9]
    amp_ref, held_ref, acc_ref, slot_ref, place_ref, amp_sem, held_sem, out_sem, acc_sem = rest[-9:]
    size = tiles_ref.shape[-1]
    lines = 1 if last else SIDE - 1
    copies = []
    if last:
        copies.append(pltpu.make_async_copy(rest[pieces_given], acc_ref, acc_sem))
    start = 0
    for i, piece in enumerate(pieces):
        rows = piece.shape[0]
        copies.append(pltpu.make_async_copy(piece, amp_ref.at[pl.ds(start, rows)], amp_sem.at[i]))
        start += rows
    for copy in copies:
        copy.start()

    me = lax.axis_index("ab")
    my_y = me >> 2
    my_x = me & 3

    def pick(k, found):
        col = col_ref[k]
        in_x = (120 >> (2 * (((col >> 1) - my_x) & 3))) & 3
        in_y = (120 >> (2 * (((col >> 3) - my_y) & 3))) & 3
        odd = col & 1
        line = jnp.where(odd == 0, in_y, in_x)
        spot = jnp.where(odd == 0, in_x, in_y)
        slot_ref[found] = k
        if last:
            place_ref[found] = odd * SIDE + spot
            return found + jnp.where(line == SIDE - 1, 1, 0)
        place_ref[found] = (odd * lines + line) * SIDE + spot
        return found + jnp.where(line == SIDE - 1, 0, 1)

    count = lax.fori_loop(0, count_ref[0], pick, 0)

    def tile_copy(j):
        spot = lax.rem(j, HELD)
        return pltpu.make_async_copy(tiles_ref.at[slot_ref[j]], held_ref.at[spot], held_sem.at[spot])

    def fetch(j):
        @pl.when(j < count)
        def _():
            tile_copy(j).start()

    for j in range(HELD):
        fetch(j)
    if not last:
        acc_ref[...] = jnp.zeros_like(acc_ref)
    for copy in copies:
        copy.wait()

    def split(value):
        high = value.astype(jnp.bfloat16)
        return high, (value - high.astype(jnp.float32)).astype(jnp.bfloat16)

    def term_of(j):
        high, low = split(amp_ref[pl.ds(pl.multiple_of(place_ref[j] * size, size), size), :])
        tile_high, tile_low = split(held_ref[lax.rem(j, HELD)])
        term = jnp.dot(tile_high, high, preferred_element_type=jnp.float32)
        term += jnp.dot(tile_high, low, preferred_element_type=jnp.float32)
        return term + jnp.dot(tile_low, high, preferred_element_type=jnp.float32)

    def add_term(j, term):
        spot = pl.multiple_of(row_ref[slot_ref[j]] * 32, 32)
        for hi in range(8):
            for c in range(CHUNKS):
                acc_ref[c, hi, pl.ds(spot, 32), :] += term[
                    hi * 32 : hi * 32 + 32, c * LANES : (c + 1) * LANES
                ]

    def add_group(g, carry):
        for i in range(GROUP):
            tile_copy(GROUP * g + i).wait()
        terms = [term_of(GROUP * g + i) for i in range(GROUP)]
        for i in range(GROUP):
            add_term(GROUP * g + i, terms[i])
        for i in range(GROUP):
            fetch(GROUP * g + i + HELD)
        return carry

    def add_one(j, carry):
        tile_copy(j).wait()
        add_term(j, term_of(j))
        return carry

    groups = count // GROUP
    lax.fori_loop(0, groups, add_group, 0)
    lax.fori_loop(groups * GROUP, count, add_one, 0)

    if not last:
        copy = pltpu.make_async_copy(acc_ref, outs[0], acc_sem)
        copy.start()
        copy.wait()
        return
    me_cd = lax.axis_index("cd")
    size_cd = acc_ref.shape[1]
    parts = out_parts(acc_ref.shape[2], size_cd)
    copies = []
    for i, (distance, first, rows) in enumerate(parts):
        block = lax.rem(me_cd + (distance + size_cd), size_cd)
        for c in range(CHUNKS):
            spot = c * len(parts) + i
            source = acc_ref.at[c, block, pl.ds(first, rows)]
            copies.append(pltpu.make_async_copy(source, outs[spot], out_sem.at[spot]))
    for copy in copies:
        copy.start()
    for copy in copies:
        copy.wait()


def ladder(tile_row, tile_col, tile_count, tiles, pieces, so_far, blocks):
    slots, size, _ = tiles.shape
    width = pieces[0].shape[1]
    total = sum(piece.shape[0] for piece in pieces)
    size_cd = lax.axis_size("cd")
    smem = pl.BlockSpec(memory_space=pltpu.SMEM)
    hbm = pl.BlockSpec(memory_space=pl.ANY)
    acc = (CHUNKS, size_cd, blocks * 32, LANES)
    if so_far:
        outs = [(rows, LANES) for _, _, rows in out_parts(blocks * 32, size_cd)] * CHUNKS
    else:
        outs = [acc]
    share = total / (2 * SIDE * SIDE * size)
    return pl.pallas_call(
        functools.partial(ladder_kernel, pieces_given=len(pieces), last=len(so_far)),
        in_specs=[smem] * 3 + [pl.BlockSpec(memory_space=pltpu.HBM)] + [hbm] * (len(pieces) + len(so_far)),
        out_specs=[hbm] * len(outs),
        out_shape=[jax.ShapeDtypeStruct(shape, jnp.float32) for shape in outs],
        scratch_shapes=[
            pltpu.VMEM((total, width), jnp.float32),
            pltpu.VMEM((HELD, size, size), jnp.float32),
            pltpu.VMEM(acc, jnp.float32),
            pltpu.SMEM((slots,), jnp.int32),
            pltpu.SMEM((slots,), jnp.int32),
            pltpu.SemaphoreType.DMA((len(pieces),)),
            pltpu.SemaphoreType.DMA((HELD,)),
            pltpu.SemaphoreType.DMA((len(outs),)),
            pltpu.SemaphoreType.DMA,
        ],
        compiler_params=pltpu.CompilerParams(vmem_limit_bytes=(14 if so_far else 18) * 1024 * 1024),
        cost_estimate=pl.CostEstimate(
            flops=int(share * slots * 6 * size * size * width),
            bytes_accessed=int(share * slots * size * size * 4)
            + total * width * 4
            + (1 + len(so_far)) * blocks * size * width * 4,
            transcendentals=0,
        ),
        name="ladder_last" if so_far else "ladder",
    )(tile_row, tile_col, tile_count, tiles, *pieces, *so_far)


def shift_line(block, step):
    size = lax.axis_size("cd")
    return lax.ppermute(block, "cd", [(i, (i + step) % size) for i in range(size)])


def ring_terms(given):
    up, down = shift_line(given[0], 1), shift_line(given[1], -1)
    half = up.shape[0]
    for step in range(2, len(given) - 1, 2):
        ahead, behind = given[step : step + 2]
        if step == 2:
            up = jnp.concatenate([ahead[:half] + up, ahead[half:]], axis=0)
            down = jnp.concatenate([behind[:half], behind[half:] + down], axis=0)
        else:
            up = ahead + up
            down = behind + down
        up = shift_line(up, 1)
        down = shift_line(down, -1)
    return [up, down, given[-1]]


def bring(refs, held_ref, sem):
    copies = [pltpu.make_async_copy(ref, held_ref.at[i], sem.at[i]) for i, ref in enumerate(refs)]
    for copy in copies:
        copy.start()
    for copy in copies:
        copy.wait()


def merge_kernel(*refs, terms):
    out_ref, held_ref, terms_ref, sem = refs[-4:]
    bring(refs[:-4], terms_ref, sem)
    start = 0
    for c in range(CHUNKS):
        value = terms_ref[start]
        for i in range(start + 1, start + terms[c]):
            value = value + terms_ref[i]
        start += terms[c]
        held_ref[...] = value
        for row in range(held_ref.shape[0] // 32):
            for a in range(2):
                for b in range(2):
                    out_ref[pl.ds(row * 64 + c * 4 + a * 2 + b, 8, stride=8), :] = held_ref[
                        pl.ds(row * 32 + a * 16 + b, 8, stride=2), :
                    ]


def merge(chunks):
    rows = chunks[0][0].shape[0]
    flat = [term for terms in chunks for term in terms]
    return pl.pallas_call(
        functools.partial(merge_kernel, terms=[len(terms) for terms in chunks]),
        in_specs=[pl.BlockSpec(memory_space=pl.ANY)] * len(flat),
        out_specs=pl.BlockSpec(memory_space=pltpu.VMEM),
        out_shape=jax.ShapeDtypeStruct((CHUNKS * rows, LANES), jnp.float32),
        scratch_shapes=[
            pltpu.VMEM((rows, LANES), jnp.float32),
            pltpu.VMEM((len(flat), rows, LANES), jnp.float32),
            pltpu.SemaphoreType.DMA((len(flat),)),
        ],
        compiler_params=pltpu.CompilerParams(vmem_limit_bytes=8 * 1024 * 1024),
        name="merge",
    )(*flat)


def finish_kernel(direct_any, mirror_any, out_ref, rows_ref, held_ref, sem):
    bring([direct_any, mirror_any], held_ref, sem)
    direct_ref, mirror_ref = held_ref.at[0], held_ref.at[1]
    for o in range(CHUNKS):
        for a in range(2):
            for b in range(2):
                rows_ref[pl.ds(b, LANES, stride=2), :] = (
                    direct_ref[pl.ds(o * 4 + a * 2 + b, LANES, stride=8), :]
                    + mirror_ref[pl.ds(o * 4 + b * 2 + a, LANES, stride=8), :]
                )
            out_ref[pl.ds(o * LANES, LANES), a, :] = rows_ref[...].T


def finish(direct, mirror):
    return pl.pallas_call(
        finish_kernel,
        in_specs=[pl.BlockSpec(memory_space=pl.ANY)] * 2,
        out_specs=pl.BlockSpec(memory_space=pltpu.VMEM),
        out_shape=jax.ShapeDtypeStruct((CHUNKS * LANES, 2, 2 * LANES), jnp.float32),
        scratch_shapes=[
            pltpu.VMEM((2 * LANES, LANES), jnp.float32),
            pltpu.VMEM((2, *direct.shape), jnp.float32),
            pltpu.SemaphoreType.DMA((2,)),
        ],
        compiler_params=pltpu.CompilerParams(vmem_limit_bytes=8 * 1024 * 1024),
        name="finish",
    )(direct, mirror)


def per_device(amplitudes, integrals, tile_row, tile_col, tile_count):
    occ_dev = amplitudes.shape[0]
    blocks = lax.axis_size("ab")

    near, far = gather_plane(amplitudes.T)
    so_far = ladder(tile_row, tile_col, tile_count, integrals, near, [], blocks)
    given = ladder(tile_row, tile_col, tile_count, integrals, far, so_far, blocks)
    each = len(given) // CHUNKS
    sums = [ring_terms(given[c * each : (c + 1) * each]) for c in range(CHUNKS)]
    direct = merge(sums)
    outgoing = direct.reshape(-1, 8, LANES)
    arrived = lax.all_to_all(outgoing, ("ab", "cd"), split_axis=0, concat_axis=0, tiled=True)
    partner = lax.ppermute(arrived, "ij", [(0, 1), (1, 0)]).reshape(direct.shape)
    return finish(direct, partner).reshape(occ_dev, 1, 2, 2 * LANES)


def solution(mesh):
    in_specs = (
        P("ij", ("cd", "ab")),
        P(("ab", "cd"), None, None),
        P(("ab", "cd")),
        P(("ab", "cd")),
        P(("ab", "cd")),
    )
    out_specs = P("ij", "ab", "cd", None)
    return jax.shard_map(
        per_device, mesh=mesh, in_specs=in_specs, out_specs=out_specs, check_vma=False
    )
```

```python
import functools

import jax
import jax.numpy as jnp
from jax import lax
from jax.experimental import pallas as pl
from jax.experimental.pallas import tpu as pltpu
from jax.sharding import PartitionSpec as P

LANES = 128
SIDE = 4
CHUNKS = 2
HELD = 16
GROUP = 4


def plane_route(dx, dy):
    route = []
    for y in range(SIDE):
        for x in range(SIDE):
            route.append((y * SIDE + x, (y + dy) % SIDE * SIDE + (x + dx) % SIDE))
    return route


def both_ways(block, dx, dy):
    return [
        lax.ppermute(block, "ab", plane_route(dx, dy)),
        lax.ppermute(block, "ab", plane_route(-dx, -dy)),
    ]


def far_halves(pair, dx, dy):
    below, above = pair
    half = below.shape[0] // 2
    return [
        lax.ppermute(below[:half], "ab", plane_route(dx, dy)),
        lax.ppermute(above[half:], "ab", plane_route(-dx, -dy)),
    ]


def first_line(block, dx, dy):
    far = lax.ppermute(block, "ab", plane_route(2 * dx, 2 * dy))
    return jnp.concatenate([block] + both_ways(block, dx, dy) + [far], axis=0)


def gather_plane(block):
    half = block.shape[0] // 2
    along_x, along_y = (1, 0), (0, 1)
    low = first_line(block[:half], *along_x)
    up = first_line(block[half:], *along_y)
    near_low = both_ways(low, *along_y)
    near_up = both_ways(up, *along_x)
    far = far_halves(near_low, *along_y) + far_halves(near_up, *along_x)
    return [low] + near_low + [up] + near_up, far


def out_parts(rows, size):
    half = rows // 2
    parts = [(size // 2, 0, half), (size // 2, half, half)]
    for distance in range(size // 2 - 1, 0, -1):
        parts += [(distance, 0, rows), (-distance, 0, rows)]
    return parts + [(0, 0, rows)]


def ladder_kernel(row_ref, col_ref, count_ref, tiles_ref, *rest, pieces_given, last):
    pieces = rest[:pieces_given]
    outs = rest[pieces_given + last : -9]
    amp_ref, held_ref, acc_ref, slot_ref, place_ref, amp_sem, held_sem, out_sem, acc_sem = rest[-9:]
    size = tiles_ref.shape[-1]
    lines = 1 if last else SIDE - 1
    copies = []
    if last:
        copies.append(pltpu.make_async_copy(rest[pieces_given], acc_ref, acc_sem))
    start = 0
    for i, piece in enumerate(pieces):
        rows = piece.shape[0]
        copies.append(pltpu.make_async_copy(piece, amp_ref.at[pl.ds(start, rows)], amp_sem.at[i]))
        start += rows
    for copy in copies:
        copy.start()

    me = lax.axis_index("ab")
    my_y = me >> 2
    my_x = me & 3

    def pick(k, found):
        col = col_ref[k]
        in_x = (120 >> (2 * (((col >> 1) - my_x) & 3))) & 3
        in_y = (120 >> (2 * (((col >> 3) - my_y) & 3))) & 3
        odd = col & 1
        line = jnp.where(odd == 0, in_y, in_x)
        spot = jnp.where(odd == 0, in_x, in_y)
        slot_ref[found] = k
        if last:
            place_ref[found] = odd * SIDE + spot
            return found + jnp.where(line == SIDE - 1, 1, 0)
        place_ref[found] = (odd * lines + line) * SIDE + spot
        return found + jnp.where(line == SIDE - 1, 0, 1)

    count = lax.fori_loop(0, count_ref[0], pick, 0)

    def tile_copy(j):
        spot = lax.rem(j, HELD)
        return pltpu.make_async_copy(tiles_ref.at[slot_ref[j]], held_ref.at[spot], held_sem.at[spot])

    def fetch(j):
        @pl.when(j < count)
        def _():
            tile_copy(j).start()

    for j in range(HELD):
        fetch(j)
    if not last:
        acc_ref[...] = jnp.zeros_like(acc_ref)
    for copy in copies:
        copy.wait()

    def split(value):
        high = value.astype(jnp.bfloat16)
        return high, (value - high.astype(jnp.float32)).astype(jnp.bfloat16)

    def term_of(j):
        high, low = split(amp_ref[pl.ds(pl.multiple_of(place_ref[j] * size, size), size), :])
        tile_high, tile_low = split(held_ref[lax.rem(j, HELD)])
        term = jnp.dot(tile_high, high, preferred_element_type=jnp.float32)
        term += jnp.dot(tile_high, low, preferred_element_type=jnp.float32)
        return term + jnp.dot(tile_low, high, preferred_element_type=jnp.float32)

    def add_term(j, term):
        spot = pl.multiple_of(row_ref[slot_ref[j]] * 32, 32)
        for hi in range(8):
            for c in range(CHUNKS):
                acc_ref[c, hi, pl.ds(spot, 32), :] += term[
                    hi * 32 : hi * 32 + 32, c * LANES : (c + 1) * LANES
                ]

    def add_group(g, carry):
        for i in range(GROUP):
            tile_copy(GROUP * g + i).wait()
        terms = [term_of(GROUP * g + i) for i in range(GROUP)]
        for i in range(GROUP):
            add_term(GROUP * g + i, terms[i])
        for i in range(GROUP):
            fetch(GROUP * g + i + HELD)
        return carry

    def add_one(j, carry):
        tile_copy(j).wait()
        add_term(j, term_of(j))
        return carry

    groups = count // GROUP
    lax.fori_loop(0, groups, add_group, 0)
    lax.fori_loop(groups * GROUP, count, add_one, 0)

    if not last:
        copy = pltpu.make_async_copy(acc_ref, outs[0], acc_sem)
        copy.start()
        copy.wait()
        return
    me_cd = lax.axis_index("cd")
    size_cd = acc_ref.shape[1]
    parts = out_parts(acc_ref.shape[2], size_cd)
    copies = []
    for i, (distance, first, rows) in enumerate(parts):
        block = lax.rem(me_cd + (distance + size_cd), size_cd)
        for c in range(CHUNKS):
            spot = c * len(parts) + i
            source = acc_ref.at[c, block, pl.ds(first, rows)]
            copies.append(pltpu.make_async_copy(source, outs[spot], out_sem.at[spot]))
    for copy in copies:
        copy.start()
    for copy in copies:
        copy.wait()


def ladder(tile_row, tile_col, tile_count, tiles, pieces, so_far, blocks):
    slots, size, _ = tiles.shape
    width = pieces[0].shape[1]
    total = sum(piece.shape[0] for piece in pieces)
    size_cd = lax.axis_size("cd")
    smem = pl.BlockSpec(memory_space=pltpu.SMEM)
    hbm = pl.BlockSpec(memory_space=pl.ANY)
    acc = (CHUNKS, size_cd, blocks * 32, LANES)
    if so_far:
        outs = [(rows, LANES) for _, _, rows in out_parts(blocks * 32, size_cd)] * CHUNKS
    else:
        outs = [acc]
    share = total / (2 * SIDE * SIDE * size)
    return pl.pallas_call(
        functools.partial(ladder_kernel, pieces_given=len(pieces), last=len(so_far)),
        in_specs=[smem] * 3 + [pl.BlockSpec(memory_space=pltpu.HBM)] + [hbm] * (len(pieces) + len(so_far)),
        out_specs=[hbm] * len(outs),
        out_shape=[jax.ShapeDtypeStruct(shape, jnp.float32) for shape in outs],
        scratch_shapes=[
            pltpu.VMEM((total, width), jnp.float32),
            pltpu.VMEM((HELD, size, size), jnp.float32),
            pltpu.VMEM(acc, jnp.float32),
            pltpu.SMEM((slots,), jnp.int32),
            pltpu.SMEM((slots,), jnp.int32),
            pltpu.SemaphoreType.DMA((len(pieces),)),
            pltpu.SemaphoreType.DMA((HELD,)),
            pltpu.SemaphoreType.DMA((len(outs),)),
            pltpu.SemaphoreType.DMA,
        ],
        compiler_params=pltpu.CompilerParams(vmem_limit_bytes=(14 if so_far else 18) * 1024 * 1024),
        cost_estimate=pl.CostEstimate(
            flops=int(share * slots * 6 * size * size * width),
            bytes_accessed=int(share * slots * size * size * 4)
            + total * width * 4
            + (1 + len(so_far)) * blocks * size * width * 4,
            transcendentals=0,
        ),
        name="ladder_last" if so_far else "ladder",
    )(tile_row, tile_col, tile_count, tiles, *pieces, *so_far)


def shift_line(block, step):
    size = lax.axis_size("cd")
    return lax.ppermute(block, "cd", [(i, (i + step) % size) for i in range(size)])


def ring_terms(given):
    up, down = shift_line(given[0], 1), shift_line(given[1], -1)
    half = up.shape[0]
    for step in range(2, len(given) - 1, 2):
        ahead, behind = given[step : step + 2]
        if step == 2:
            up = jnp.concatenate([ahead[:half] + up, ahead[half:]], axis=0)
            down = jnp.concatenate([behind[:half], behind[half:] + down], axis=0)
        else:
            up = ahead + up
            down = behind + down
        up = shift_line(up, 1)
        down = shift_line(down, -1)
    return [up, down, given[-1]]


def bring(refs, held_ref, sem):
    copies = [pltpu.make_async_copy(ref, held_ref.at[i], sem.at[i]) for i, ref in enumerate(refs)]
    for copy in copies:
        copy.start()
    for copy in copies:
        copy.wait()


def merge_kernel(*refs, terms):
    out_ref, held_ref, terms_ref, sem = refs[-4:]
    bring(refs[:-4], terms_ref, sem)
    start = 0
    for c in range(CHUNKS):
        value = terms_ref[start]
        for i in range(start + 1, start + terms[c]):
            value = value + terms_ref[i]
        start += terms[c]
        held_ref[...] = value
        for row in range(held_ref.shape[0] // 32):
            for a in range(2):
                for b in range(2):
                    out_ref[pl.ds(row * 64 + c * 4 + a * 2 + b, 8, stride=8), :] = held_ref[
                        pl.ds(row * 32 + a * 16 + b, 8, stride=2), :
                    ]


def merge(chunks):
    rows = chunks[0][0].shape[0]
    flat = [term for terms in chunks for term in terms]
    return pl.pallas_call(
        functools.partial(merge_kernel, terms=[len(terms) for terms in chunks]),
        in_specs=[pl.BlockSpec(memory_space=pl.ANY)] * len(flat),
        out_specs=pl.BlockSpec(memory_space=pltpu.VMEM),
        out_shape=jax.ShapeDtypeStruct((CHUNKS * rows, LANES), jnp.float32),
        scratch_shapes=[
            pltpu.VMEM((rows, LANES), jnp.float32),
            pltpu.VMEM((len(flat), rows, LANES), jnp.float32),
            pltpu.SemaphoreType.DMA((len(flat),)),
        ],
        compiler_params=pltpu.CompilerParams(vmem_limit_bytes=8 * 1024 * 1024),
        name="merge",
    )(*flat)


def finish_kernel(direct_any, mirror_any, out_ref, rows_ref, held_ref, sem):
    bring([direct_any, mirror_any], held_ref, sem)
    direct_ref, mirror_ref = held_ref.at[0], held_ref.at[1]
    for o in range(CHUNKS):
        for a in range(2):
            for b in range(2):
                rows_ref[pl.ds(b, LANES, stride=2), :] = (
                    direct_ref[pl.ds(o * 4 + a * 2 + b, LANES, stride=8), :]
                    + mirror_ref[pl.ds(o * 4 + b * 2 + a, LANES, stride=8), :]
                )
            out_ref[pl.ds(o * LANES, LANES), a, :] = rows_ref[...].T


def finish(direct, mirror):
    return pl.pallas_call(
        finish_kernel,
        in_specs=[pl.BlockSpec(memory_space=pl.ANY)] * 2,
        out_specs=pl.BlockSpec(memory_space=pltpu.VMEM),
        out_shape=jax.ShapeDtypeStruct((CHUNKS * LANES, 2, 2 * LANES), jnp.float32),
        scratch_shapes=[
            pltpu.VMEM((2 * LANES, LANES), jnp.float32),
            pltpu.VMEM((2, *direct.shape), jnp.float32),
            pltpu.SemaphoreType.DMA((2,)),
        ],
        compiler_params=pltpu.CompilerParams(vmem_limit_bytes=8 * 1024 * 1024),
        name="finish",
    )(direct, mirror)


def per_device(amplitudes, integrals, tile_row, tile_col, tile_count):
    occ_dev = amplitudes.shape[0]
    blocks = lax.axis_size("ab")

    near, far = gather_plane(amplitudes.T)
    so_far = ladder(tile_row, tile_col, tile_count, integrals, near, [], blocks)
    given = ladder(tile_row, tile_col, tile_count, integrals, far, so_far, blocks)
    each = len(given) // CHUNKS
    sums = [ring_terms(given[c * each : (c + 1) * each]) for c in range(CHUNKS)]
    direct = merge(sums)
    outgoing = direct.reshape(-1, 8, LANES)
    arrived = lax.all_to_all(outgoing, ("ab", "cd"), split_axis=0, concat_axis=0, tiled=True)
    partner = lax.ppermute(arrived, "ij", [(0, 1), (1, 0)]).reshape(direct.shape)
    return finish(direct, partner).reshape(occ_dev, 1, 2, 2 * LANES)


def solution(mesh):
    in_specs = (
        P("ij", ("cd", "ab")),
        P(("ab", "cd"), None, None),
        P(("ab", "cd")),
        P(("ab", "cd")),
        P(("ab", "cd")),
    )
    out_specs = P("ij", "ab", "cd", None)
    return jax.shard_map(
        per_device, mesh=mesh, in_specs=in_specs, out_specs=out_specs, check_vma=False
    )
```
